1024 devices in a mesh: grp: 128 (over z, y, core), mem: 8 (over x).
Axes of the slice: x: 8, y: 8, z: 8, core: 2. Of those that a mesh axis runs over, the one named last changes fastest.
Arguments:
- wave: float32 [2, 512, 256, 256], P(None, 'grp', 'mem'), may hold values from -6 to 6
- beam_offsets: float32 [3, 128, 8, 1024], P(None, 'grp', 'mem'), may hold values from 0 to 1
- beam_waves: float32 [3, 128, 8, 1024], P(None, 'grp', 'mem'), may hold values from -3.140625 to 3.140625
- beam_amps: float32 [2, 128, 8, 1024], P(None, 'grp', 'mem'), may hold values from -6 to 6
- beam_widths: float32 [128, 8, 1024], P('grp', 'mem'), may hold values from 1.2 to 3
- beam_tile: int32 [128, 8, 1024], P('grp', 'mem'), may hold values from 0 to 31
- send_list: int32 [128, 8, 1024], P('grp', 'mem'), may hold values from 0 to 1023, each once within a row
- send_count: int32 [128, 8, 128], P('grp', 'mem'), may hold values from 1 to 8, as said below
Outputs:
- wave_out: float32 [2, 512, 256, 256], P(None, 'grp', 'mem')
- potential: float32 [256, 128, 128], P('grp', 'mem')
The draws below stay inside these ranges and needn't reach their ends.
Inputs may be any that keep to these rules, and one draw needn't show every extreme that they name: `send_list`: each device's list names each of its 1024 beams once. `send_count`: every device fills all 8 slots toward some group.
All inputs are finite; a program needn't handle non-finite values.
Results may differ from the reference program's by a relative error of at most 0.0003.
Values sent between devices are 32-bit elements; how exact they have to be, the bound alone decides.
A program may use at most 64 MiB of HBM per device.

```python
import math
import jax
import jax.numpy as jnp
from jax import lax

GX = 128
GY = 128
CZ = 2
TILE = 16
CAP = 8
STEPS = 1
GROUPS = 128
MEMBERS = 8
FX = 256
FY = 256
FZ = 512
BEAM_DEV = 1024
TILES_DEV = 32
N_GRP = 128
N_MEM = 8


def draw_send_count(key, part):
    key_level, key_spread, key_full = jax.random.split(jax.random.fold_in(key, 11), 3)
    levels = jax.random.randint(key_level, (1, 1, GROUPS), 1, CAP + 1)
    spread = jax.random.randint(key_spread, (GROUPS, MEMBERS, GROUPS), 0, CAP)
    counts = 1 + spread % levels
    chosen = jax.random.randint(key_full, (GROUPS, MEMBERS, 1), 0, GROUPS)
    filled = jnp.arange(GROUPS)[None, None, :] == chosen
    return jnp.where(filled, CAP, counts).astype(jnp.int32)


def plant(result, rng, low, high):
    place = [jax.random.randint(jax.random.fold_in(rng, axis), (), 0, length) for axis, length in enumerate(result.shape)]
    longest = result.shape.index(max(result.shape))
    beside = place[:longest] + [(place[longest] + 1) % result.shape[longest]] + place[longest + 1:]
    return result.at[tuple(place)].set(low).at[tuple(beside)].set(high)


def shard_levels(own_key, shape, pieces, least, high):
    factor_of, own = 1.0, jax.random.fold_in(own_key, 6)
    for axis_at, shards_of in pieces:
        draws = jnp.exp(jax.random.uniform(jax.random.fold_in(own, axis_at), (shards_of,), jnp.float32, least / len(pieces), high / len(pieces)))
        factor_of = factor_of * jnp.repeat(draws, shape[axis_at] // shards_of).reshape([-1 if axis == axis_at else 1 for axis in range(len(shape))])
    return factor_of


def scatter_about(stream_key, dims, deviation, limit, shards=(), kind=jnp.bfloat16):
    factor_of = shard_levels(stream_key, dims, shards, -0.22, 0.18) if shards else 1.0
    values = jax.random.normal(stream_key, dims, jnp.float32) * deviation * factor_of
    return jnp.minimum(jnp.maximum(values, -limit), limit).astype(kind)


def setup_inputs(seed: int = 0) -> dict:
    keys = jax.random.split(jax.random.key(seed), 9)
    return {
        "wave": scatter_about(keys[0], (2, FZ, FX, FY), 1.0, 6.0, ((1, 128), (2, 8)), jnp.float32),
        "beam_offsets": jnp.clip(1.0 * jax.random.uniform(keys[1], (3, GROUPS, MEMBERS, BEAM_DEV), jnp.float32) ** shard_levels(keys[1], (3, GROUPS, MEMBERS, BEAM_DEV), ((1, 128), (2, 8)), -0.2, 0.2), 0.0, 1.0),
        "beam_waves": jnp.clip(jax.random.uniform(keys[2], (3, GROUPS, MEMBERS, BEAM_DEV), jnp.float32, -3.140625, 3.140625), -3.140625, 3.140625),
        "beam_amps": scatter_about(keys[3], (2, GROUPS, MEMBERS, BEAM_DEV), 1.0, 6.0, ((1, 128), (2, 8)), jnp.float32),
        "beam_widths": jnp.clip(jnp.exp(math.log(3.0) - 0.9162907 * jax.random.uniform(keys[4], (GROUPS, MEMBERS, BEAM_DEV), jnp.float32) ** shard_levels(keys[4], (GROUPS, MEMBERS, BEAM_DEV), ((0, 128), (1, 8)), -0.2, 0.2)), 1.2, 3.0),
        "beam_tile": plant(jax.random.randint(keys[5], (GROUPS, MEMBERS, BEAM_DEV), 0, TILES_DEV), jax.random.fold_in(keys[5], 1), 0, TILES_DEV - 1).astype(jnp.int32),
        "send_list": jax.vmap(lambda own: jax.random.permutation(own, BEAM_DEV))(jax.random.split(keys[6], GROUPS * MEMBERS)).reshape((GROUPS, MEMBERS, BEAM_DEV)).astype(jnp.int32),
        "send_count": draw_send_count(jax.random.fold_in(keys[8], 71), 0),
    }


GRAV = 0.005
SCREEN = 0.0004
STEP_TIME = 0.2
HIGHEST = lax.Precision.HIGHEST


def profile(coords, centre, breadth, wavenum):
    offset = coords[None, :] - centre[:, None]
    envelope = jnp.exp(-(offset * offset) / (2.0 * breadth[:, None] * breadth[:, None]))
    phases = wavenum[:, None] * offset
    return envelope * jnp.cos(phases), envelope * jnp.sin(phases)


def deposit(params, planes, columns, length):
    number = params.shape[1]
    z_real, z_imag = profile(jnp.arange(planes).astype(jnp.float32), params[0], params[8], params[3])
    x_real, x_imag = profile(jnp.arange(columns).astype(jnp.float32), params[1], params[8], params[4])
    y_real, y_imag = profile(jnp.arange(length).astype(jnp.float32), params[2], params[8], params[5])
    amp_real = params[6][:, None]
    amp_imag = params[7][:, None]
    az_real = amp_real * z_real - amp_imag * z_imag
    az_imag = amp_real * z_imag + amp_imag * z_real
    left_real = (az_real[:, :, None] * x_real[:, None, :] - az_imag[:, :, None] * x_imag[:, None, :]).reshape(number, planes * columns)
    left_imag = (az_real[:, :, None] * x_imag[:, None, :] + az_imag[:, :, None] * x_real[:, None, :]).reshape(number, planes * columns)
    part_rr = jnp.einsum("bk,by->ky", left_real, y_real, precision=HIGHEST)
    part_ii = jnp.einsum("bk,by->ky", left_imag, y_imag, precision=HIGHEST)
    part_ri = jnp.einsum("bk,by->ky", left_real, y_imag, precision=HIGHEST)
    part_ir = jnp.einsum("bk,by->ky", left_imag, y_real, precision=HIGHEST)
    return jnp.stack([part_rr - part_ii, part_ri + part_ir]).reshape(2, planes, columns, length)


def centres(beam_offsets, beam_waves, beam_amps, beam_widths, beam_tile, planes, length):
    tiles_y = length // TILE
    tile_x = (beam_tile // tiles_y).astype(jnp.float32)
    tile_y = (beam_tile % tiles_y).astype(jnp.float32)
    centre_z = beam_offsets[0] * float(planes)
    centre_x = TILE * tile_x + TILE * beam_offsets[1]
    centre_y = TILE * tile_y + TILE * beam_offsets[2]
    return jnp.stack([centre_z, centre_x, centre_y, beam_waves[0], beam_waves[1], beam_waves[2], beam_amps[0], beam_amps[1], beam_widths])


def eigen_at(indices, number):
    return 2.0 * jnp.cos((2.0 * math.pi / number) * indices.astype(jnp.float32)) - 2.0


def laplace(field):
    beside_all = jnp.roll(field, 1, 1) + jnp.roll(field, -1, 1) + jnp.roll(field, 1, 2) + jnp.roll(field, -1, 2) + jnp.roll(field, 1, 3) + jnp.roll(field, -1, 3)
    return beside_all - 6.0 * field


def drift(field, fine_pot):
    spread = laplace(field)
    return jnp.stack([-(0.5 * spread[1] - fine_pot * field[1]), 0.5 * spread[0] - fine_pot * field[0]])


def reference(wave, beam_offsets, beam_waves, beam_amps, beam_widths, beam_tile, send_list, send_count):
    planes = 2 * CZ
    columns = 2 * GX // N_MEM
    length = 2 * GY
    params = centres(beam_offsets, beam_waves, beam_amps, beam_widths, beam_tile, planes, length)

    def one_block(target):
        group_index = target // N_MEM
        member = target % N_MEM
        member_lists = lax.dynamic_index_in_dim(send_list, member, 1, keepdims=False)
        chosen = lax.dynamic_slice_in_dim(member_lists, group_index * CAP, CAP, 1)
        counts = lax.dynamic_index_in_dim(lax.dynamic_index_in_dim(send_count, member, 1, keepdims=False), group_index, 1, keepdims=False)
        source = lax.dynamic_index_in_dim(params, member, 2, keepdims=False)
        picked = jnp.take_along_axis(source, chosen[None], axis=2)
        sent_mask = (jnp.arange(CAP, dtype=jnp.int32)[None, :] < counts[:, None]).astype(jnp.float32)
        picked = jnp.concatenate([picked[:6], picked[6:8] * sent_mask[None], picked[8:]], axis=0)
        return deposit(picked.reshape(9, N_GRP * CAP), planes, columns, length)

    blocks = lax.map(one_block, jnp.arange(N_GRP * N_MEM, dtype=jnp.int32))
    blocks = blocks.reshape(N_GRP, N_MEM, 2, planes, columns, length)
    deposited = blocks.transpose(2, 0, 3, 1, 4, 5).reshape(2, N_GRP * planes, N_MEM * columns, length)
    field_now = wave + deposited

    density = field_now[0] * field_now[0] + field_now[1] * field_now[1]
    full_z = N_GRP * CZ
    coarse = density.reshape(full_z, 2, GX, 2, GY, 2).mean(axis=(1, 3, 5))
    spectrum = jnp.fft.fftn(coarse)
    wave_z = jnp.arange(full_z, dtype=jnp.int32)
    wave_x = jnp.arange(GX, dtype=jnp.int32)
    wave_y = jnp.arange(GY, dtype=jnp.int32)
    eigenvalues = eigen_at(wave_z, full_z)[:, None, None] + eigen_at(wave_x, GX)[None, :, None] + eigen_at(wave_y, GY)[None, None, :]
    zero_mode = (wave_z == 0)[:, None, None] & (wave_x == 0)[None, :, None] & (wave_y == 0)[None, None, :]
    factor = jnp.where(zero_mode, 0.0, 1.0 / (eigenvalues - SCREEN))
    potential = GRAV * jnp.real(jnp.fft.ifftn(spectrum * factor))

    fine_pot = jnp.repeat(jnp.repeat(jnp.repeat(potential, 2, 0), 2, 1), 2, 2)
    for stepping in range(STEPS):
        slope_one = drift(field_now, fine_pot)
        slope_two = drift(field_now + (0.5 * STEP_TIME) * slope_one, fine_pot)
        slope_three = drift(field_now + (0.5 * STEP_TIME) * slope_two, fine_pot)
        slope_four = drift(field_now + STEP_TIME * slope_three, fine_pot)
        field_now = field_now + (STEP_TIME / 6.0) * (slope_one + 2.0 * slope_two + 2.0 * slope_three + slope_four)
    return field_now, potential
```

```python
import functools
import math

import jax
import jax.numpy as jnp
import numpy as np
from jax import lax
from jax.experimental import pallas as pl
from jax.experimental.pallas import tpu as pltpu
from jax.sharding import PartitionSpec as P


F32 = jnp.float32
BF16 = jnp.bfloat16
HIGHEST = lax.Precision.HIGHEST
MESH = pl.DeviceIdType.MESH

GRAV = 0.005
SCREEN = 0.0004
STEP_TIME = 0.2

G = 128
M = 8
SLOTS = 8
PLANES = 4
COLS = 32
NY = 256
BEAMS = 1024
PAD = 8
EXT_Z = PLANES + 8
EXT_X = COLS + 2 * PAD
PLANE_ROWS = ((0, 0, 24), (1, 24, 24), (-1, 48, 24), (2, 72, 24), (-2, 96, 16), (3, 112, 16))


def basis(number):
    half = number // 2
    at = np.arange(number)
    waves = np.concatenate([np.arange(half + 1), np.arange(1, half)])
    angles = 2.0 * np.pi / number * (waves[:, None] * at[None, :] % number)
    vectors = np.where(np.arange(number)[:, None] <= half, np.cos(angles), np.sin(angles))
    return vectors, (vectors**2).sum(1), 2.0 * np.cos(2.0 * np.pi / number * waves) - 2.0


@functools.cache
def tables():
    vec_y, len_y, eig_y = basis(128)
    vec_x, len_x, eig_x = vec_y, len_y, eig_y
    wz = np.arange(128)
    at = np.arange(256)
    ang = 2.0 * np.pi / 256 * (wz[:, None] * at[None, :] % 256)
    second = np.sin(ang)
    second[0] = np.cos(np.pi * at)
    vec_z = np.concatenate([np.cos(ang), second])
    len_z = (vec_z**2).sum(1)
    lam = 2.0 * np.cos(2.0 * np.pi / 256 * wz) - 2.0
    lam_second = lam.copy()
    lam_second[0] = -4.0
    eig_z = np.concatenate([lam, lam_second])

    fwd_y = np.repeat(vec_y, 2, axis=1)
    fwd_z = np.concatenate([vec_z[:, 0::2], vec_z[:, 1::2]], axis=1).T
    fwd_x = vec_x
    inv_x = np.zeros((128, 128))
    shift = np.zeros(128)
    for offset, first, rows in PLANE_ROWS:
        margin = (rows - 16) // 2
        where = (np.arange(rows) - margin) % 128
        inv_x[first : first + rows] = (vec_x / len_x[:, None])[:, where].T
        shift[first : first + rows] = offset
    turn = 2.0 * np.pi / 256 * wz[None, :] * shift[:, None]
    rot_c, rot_s = np.cos(turn), np.sin(turn)
    rot_d = rot_c.copy()
    rot_d[:, 0] = np.cos(np.pi * shift)
    inv_z = (vec_z / len_z[:, None])[:, 0::2].T
    inv_y = (vec_y / len_y[:, None]).copy()
    inv_y = np.concatenate([np.repeat(inv_y, 2, axis=1), inv_y], axis=1)
    lam_xz = eig_x[:, None] + eig_z[None, :] - SCREEN
    lam_y = np.broadcast_to(eig_y[:, None, None], (128, 1, 256))
    many = (fwd_y, fwd_z, fwd_x, inv_x, rot_c, rot_s, rot_d, inv_z, inv_y, lam_xz, lam_y)
    return tuple(np.ascontiguousarray(t, dtype=np.float32) for t in many)


SIN = tuple((-1.0) ** i / math.factorial(2 * i + 1) for i in range(6))
COS = tuple((-1.0) ** i / math.factorial(2 * i) for i in range(7))
TURN_HIGH = 6.28125
TURN_LOW = 2.0 * math.pi - TURN_HIGH


def cos_sin(phase):
    turns = jnp.round(phase * (0.5 / math.pi))
    half = 0.5 * ((phase - turns * TURN_HIGH) - turns * TURN_LOW)
    square = half * half
    sine = SIN[-1]
    for c in SIN[-2::-1]:
        sine = sine * square + c
    sine = sine * half
    cosine = COS[-1]
    for c in COS[-2::-1]:
        cosine = cosine * square + c
    return 1.0 - 2.0 * (sine * sine), 2.0 * (sine * cosine)


def parts(value):
    high = value.astype(BF16)
    return high, (value - high.astype(F32)).astype(BF16)


def dot(a, b):
    return jnp.dot(a, b, precision=HIGHEST, preferred_element_type=F32)


def dot_t(a, b, precision=HIGHEST):
    dims = (((1,), (1,)), ((), ()))
    return lax.dot_general(a, b, dims, precision=precision, preferred_element_type=F32)


def iota(shape, dim):
    return lax.broadcasted_iota(jnp.int32, shape, dim)


N_TAB = 11
TAB_SHAPES = (
    (128, 256), (256, 256), (128, 128), (128, 128), (128, 128), (128, 128), (128, 128),
    (128, 256), (128, 384), (128, 256), (1, 256),
)
ARG_SHAPES = (
    ((2, PLANES, COLS, NY), F32), ((3, 1, BEAMS), F32), ((3, 1, BEAMS), F32), ((2, 1, BEAMS), F32),
    ((1, BEAMS), F32), ((1, BEAMS), jnp.int32), ((1, BEAMS), jnp.int32), ((1, G), jnp.int32),
)
N_ARG = len(ARG_SHAPES)


def kernel(*refs):
    args_hbm, refs = refs[:N_ARG], refs[N_ARG:]
    tabs_hbm, refs = refs[:N_TAB], refs[N_TAB:]
    wave_out, pot_out = refs[:2]
    refs = refs[2:]
    args_v, refs = refs[:N_ARG], refs[N_ARG:]
    tabs_v, refs = refs[:N_TAB], refs[N_TAB:]
    (
        rows_v, one_v, two_v, send1, recv1, send2, recv2, send3, recv3, own_x, all_x,
        left_h, left_l, right_h, right_l, dens_v, pot_v, field_a, field_b, out_v, pot_c,
        arg_sem, tab_sem, out_sem, s_sem, r_sem, xs_sem, xr_sem, hs_sem, hr_sem,
    ) = refs
    wave_v, off_v, wav_v, amp_v, wid_v, til_v, sl_v, cnt_v = args_v
    (fwd_y, fwd_z, fwd_x, inv_x, rot_c, rot_s, rot_d, inv_z, inv_y, lam_xz, lam_y) = tabs_v

    g = lax.axis_index("grp")
    m = lax.axis_index("mem")
    barrier = pltpu.get_barrier_semaphore()

    def greet(j, carry):
        pl.semaphore_signal(
            barrier, inc=1, device_id=(lax.rem(g + j, G), m), device_id_type=MESH
        )
        return carry

    lax.fori_loop(1, G, greet, 0)
    for j in range(1, M):
        pl.semaphore_signal(
            barrier, inc=1, device_id=(g, lax.rem(m + j, M)), device_id_type=MESH
        )
    up, down = lax.rem(g + 1, G), lax.rem(g + G - 1, G)
    right, left = lax.rem(m + 1, M), lax.rem(m + M - 1, M)
    for corner in ((up, right), (up, left), (down, right), (down, left)):
        pl.semaphore_signal(barrier, inc=1, device_id=corner, device_id_type=MESH)

    arg_copies = [
        pltpu.make_async_copy(args_hbm[i], args_v[i], arg_sem.at[i]) for i in range(N_ARG)
    ]
    for i in (6, 5, 1, 2, 3, 4, 7, 0):
        arg_copies[i].start()
    tab_copies = []
    for i in range(N_TAB):
        source = tabs_hbm[i].at[g] if i == N_TAB - 1 else tabs_hbm[i]
        tab_copies.append(pltpu.make_async_copy(source, tabs_v[i], tab_sem.at[i]))
        tab_copies[i].start()

    arg_copies[6].wait()
    listed = jnp.broadcast_to(sl_v[...], (SLOTS, BEAMS))
    mine = (iota((SLOTS, BEAMS), 1) & (SLOTS - 1)) == iota((SLOTS, BEAMS), 0)
    listed = jnp.concatenate(
        [jnp.where(mine, listed >> 5, 0), jnp.where(mine, listed & 31, 0)], axis=0
    )
    spread = (iota((BEAMS, G), 0) >> 3) == iota((BEAMS, G), 1)
    found = jnp.dot(
        listed.astype(F32).astype(BF16),
        jnp.where(spread, 1.0, 0.0).astype(BF16),
        preferred_element_type=F32,
    )
    by_slot = (found[:SLOTS] * 32.0 + found[SLOTS:]).astype(jnp.int32)

    for i in (1, 2, 3, 4, 5, 7):
        arg_copies[i].wait()
    tile = til_v[...]
    rows_v[...] = jnp.zeros_like(rows_v)
    rows_v[0:1, :] = off_v[0] * float(PLANES)
    rows_v[1:2, :] = 16.0 * (tile >> 4).astype(F32) + 16.0 * off_v[1]
    rows_v[2:3, :] = 16.0 * (tile & 15).astype(F32) + 16.0 * off_v[2]
    for d in range(3):
        rows_v[3 + d : 4 + d, :] = wav_v[d]
    rows_v[6:7, :] = amp_v[0]
    rows_v[7:8, :] = amp_v[1]
    rows_v[8:9, :] = wid_v[...]
    exact = rows_v[...]
    first, rest = parts(exact)
    second = rest
    third = ((exact - first.astype(F32)) - second.astype(F32)).astype(BF16)
    three = jnp.concatenate([first, second, third], axis=0)
    for c in range(SLOTS):
        chosen = iota((BEAMS, G), 0) == by_slot[c : c + 1, :]
        picked = jnp.dot(
            three, jnp.where(chosen, 1.0, 0.0).astype(BF16), preferred_element_type=F32
        )
        one_v[pl.ds(c, 16, stride=SLOTS), :] = picked[0:16] + picked[16:32] + picked[32:48]
    filled = iota((SLOTS, G), 0) < cnt_v[...]
    for p in (6, 7):
        rows = slice(p * SLOTS, (p + 1) * SLOTS)
        one_v[rows, :] = jnp.where(filled, one_v[rows, :], 0.0)
    send1[:, 0, :] = one_v[...].T

    pl.semaphore_wait(barrier, (G - 1) + (M - 1) + 4)

    def scatter(source, target, number):
        def one(j, carry):
            h = lax.rem(g + j, G)
            pltpu.make_async_remote_copy(
                src_ref=source.at[h],
                dst_ref=target.at[g],
                send_sem=s_sem.at[number],
                recv_sem=r_sem.at[number],
                device_id=(h, m),
                device_id_type=MESH,
            ).start()
            return carry

        lax.fori_loop(1, G, one, 0)
        target[g] = source[g]

    def others(ref):
        return ref.at[pl.ds(0, G - 1)]

    def arrived(target, number):
        pltpu.make_async_copy(others(target), others(target), r_sem.at[number]).wait()

    def left_behind(source, number):
        pltpu.make_async_copy(others(source), others(source), s_sem.at[number]).wait()

    scatter(send1, recv1, 0)
    arrived(recv1, 0)

    two_v[...] = recv1[:, 0, :].T

    def profiles(c, carry):
        def row(p):
            return two_v[pl.ds(p * SLOTS + c, 1), :]

        width = row(8)
        scale = -0.5 / (width * width)
        at = pl.multiple_of(c * 256, 256)
        low, high = pl.ds(at, 128), pl.ds(at + 128, 128)

        away = iota((8, G), 0).astype(F32) - row(0)
        bell = jnp.exp(away * away * scale)
        cosine, sine = cos_sin(row(3) * away)
        z_r, z_i = bell * cosine, bell * sine
        a_r, a_i = row(6), row(7)
        az_r, az_i = a_r * z_r - a_i * z_i, a_r * z_i + a_i * z_r

        away = iota((COLS, G), 0).astype(F32) - row(1)
        bell = jnp.exp(away * away * scale)
        cosine, sine = cos_sin(row(4) * away)
        x_r, x_i = bell * cosine, bell * sine
        for z in range(PLANES):
            p_r, p_i = az_r[z : z + 1], az_i[z : z + 1]
            real, imag = p_r * x_r - p_i * x_i, p_r * x_i + p_i * x_r
            real_h, real_l = parts(real)
            imag_h, imag_l = parts(imag)
            top = slice(z * COLS, (z + 1) * COLS)
            bottom = slice(128 + z * COLS, 128 + (z + 1) * COLS)
            left_h[top, low] = real_h
            left_l[top, low] = real_l
            left_h[top, high] = -imag_h
            left_l[top, high] = -imag_l
            left_h[bottom, low] = imag_h
            left_l[bottom, low] = imag_l
            left_h[bottom, high] = real_h
            left_l[bottom, high] = real_l

        c_y, k_y = row(2), row(5)
        step = iota((16, G), 0).astype(F32)
        coarse_c, coarse_s = cos_sin(k_y * (16.0 * step - c_y))
        fine_c, fine_s = cos_sin(k_y * step)
        for a in range(16):
            away = (step + 16.0 * a) - c_y
            bell = jnp.exp(away * away * scale)
            b_c, b_s = coarse_c[a : a + 1], coarse_s[a : a + 1]
            real_h, real_l = parts(bell * (b_c * fine_c - b_s * fine_s))
            imag_h, imag_l = parts(bell * (b_s * fine_c + b_c * fine_s))
            rows = slice(16 * a, 16 * a + 16)
            right_h[rows, low] = real_h
            right_l[rows, low] = real_l
            right_h[rows, high] = imag_h
            right_l[rows, high] = imag_l
        return carry

    lax.fori_loop(0, SLOTS, profiles, 0)
    deposited = (
        dot_t(left_h[...], right_h[...], None)
        + dot_t(left_l[...], right_h[...], None)
        + dot_t(left_h[...], right_l[...], None)
    )
    arg_copies[0].wait()
    own_z, own_cols = pl.ds(4, PLANES), pl.ds(PAD, COLS)
    for z in range(PLANES):
        for part in range(2):
            rows = slice(part * 128 + z * COLS, part * 128 + (z + 1) * COLS)
            field_a[part, 4 + z, own_cols, :] = wave_v[part, z] + deposited[rows]
    for z in range(2):
        total = None
        for plane in (4 + 2 * z, 5 + 2 * z):
            for part in range(2):
                value = field_a[part, plane, own_cols, :]
                total = value * value if total is None else total + value * value
        for side in range(2):
            dens_v[side, z * COLS : (z + 1) * COLS, :] = total[:, side * 128 : (side + 1) * 128]
    pooled = [
        dens_v[side, pl.ds(0, COLS, stride=2), :] + dens_v[side, pl.ds(1, COLS, stride=2), :]
        for side in range(2)
    ]
    pooled = jnp.concatenate(pooled, axis=1)

    for copy in tab_copies:
        copy.wait()
    pooled = jnp.concatenate([pooled, jnp.zeros((96, NY), F32)], axis=0)
    send2[:, 0, :] = dot_t(fwd_y[...], pooled)
    scatter(send2, recv2, 1)

    first_cols, last_cols = pl.ds(PAD, 8), pl.ds(PAD + COLS - 8, 8)
    low_cols, high_cols = pl.ds(0, 8), pl.ds(PAD + COLS, 8)
    low_z, high_z = pl.ds(0, 4), pl.ds(8, 4)
    margin = []
    for i, (who, there_z, here_x, there_x) in enumerate(
        (
            ((up, m), low_z, own_cols, own_cols),
            ((down, m), high_z, own_cols, own_cols),
            ((g, right), own_z, last_cols, low_cols),
            ((g, left), own_z, first_cols, high_cols),
            ((up, right), low_z, last_cols, low_cols),
            ((up, left), low_z, first_cols, high_cols),
            ((down, right), high_z, last_cols, low_cols),
            ((down, left), high_z, first_cols, high_cols),
        )
    ):
        copy = pltpu.make_async_remote_copy(
            src_ref=field_a.at[:, own_z, here_x, :],
            dst_ref=field_a.at[:, there_z, there_x, :],
            send_sem=hs_sem.at[i],
            recv_sem=hr_sem.at[i],
            device_id=who,
            device_id_type=MESH,
        )
        copy.start()
        margin.append(copy)

    arrived(recv2, 1)
    turned = recv2[:, 0, :].T
    columns = jnp.concatenate([turned[0:16], turned[16:32]], axis=1)
    spectrum = dot(columns, fwd_z[...])
    own_x[...] = spectrum
    gathers = []
    for j in range(1, M):
        copy = pltpu.make_async_remote_copy(
            src_ref=own_x,
            dst_ref=all_x.at[j],
            send_sem=xs_sem.at[j],
            recv_sem=xr_sem.at[j],
            device_id=(g, lax.rem(m + M - j, M)),
            device_id_type=MESH,
        )
        copy.start()
        gathers.append(copy)
    all_x[0] = spectrum
    zero_mode = (iota((128, 256), 0) == 0) & (iota((128, 256), 1) == 0) & (g == 0)
    factor = jnp.where(zero_mode, 0.0, (GRAV / 8.0) / (lam_xz[...] + lam_y[...]))
    for copy in gathers:
        copy.wait_recv()
    filtered = dot(fwd_x[...], all_x[...].reshape(128, 256)) * factor
    wanted = dot(inv_x[...], filtered)
    even, odd = wanted[:, :128], wanted[:, 128:]
    moved = jnp.concatenate(
        [rot_c[...] * even + rot_s[...] * odd, rot_d[...] * odd - rot_s[...] * even], axis=1
    )
    send3[:, 0, :] = dot_t(inv_z[...], moved)
    scatter(send3, recv3, 2)
    arrived(recv3, 2)

    pot_wide = dot(recv3[:, 0, :].T, inv_y[...])
    pot_c[0] = pot_wide[4:20, NY:]
    pot_c[1] = pot_wide[28:44, NY:]
    pot_copy = pltpu.make_async_copy(pot_c, pot_out, out_sem.at[0])
    pot_copy.start()
    for edge in (0, 5):
        pot_v[edge] = jnp.full((2, EXT_X, 128), 3.0, F32)
    for offset, start, rows in PLANE_ROWS:
        block = pot_wide[start : start + rows, :NY] + 3.0
        skip = (24 - rows) // 2 * 2
        for odd_row in range(2):
            for side in range(2):
                half = block[:, side * 128 : (side + 1) * 128]
                pot_v[offset + 2, side, pl.ds(skip + odd_row, rows, stride=2), :] = half

    for copy in margin:
        copy.wait_recv()

    def stage(source, target, length, z, rows):
        top = 0 if rows is None else PAD
        count = EXT_X if rows is None else COLS
        keep = pl.ds(top, count)
        three_plus = jnp.concatenate(
            [pot_v[z // 2, 0, keep, :], pot_v[z // 2, 1, keep, :]], axis=1
        )
        sums, centres = [], []
        for part in range(2):
            whole = source[part, z]
            beside = pltpu.roll(whole, 1, 0) + pltpu.roll(whole, EXT_X - 1, 0)
            centre = source[part, z, keep, :]
            total = (
                (source[part, z - 1, keep, :] + source[part, z + 1, keep, :])
                + beside[top : top + count]
                + (pltpu.roll(centre, 1, 1) + pltpu.roll(centre, NY - 1, 1))
            )
            sums.append(0.5 * total)
            centres.append(centre)
        real = three_plus * centres[1] - sums[1]
        imag = sums[0] - three_plus * centres[0]
        new_real = field_a[0, z, keep, :] + length * real
        new_imag = field_a[1, z, keep, :] + length * imag
        if rows is None:
            target[0, z] = new_real
            target[1, z] = new_imag
        else:
            target[0, z - 4] = new_real
            target[1, z - 4] = new_imag


    def run(source, target, length, margin_z, rows=None):
        def one(z, carry):
            stage(source, target, length, z, rows)
            return carry

        lax.fori_loop(margin_z, EXT_Z - margin_z, one, 0)

    run(field_a, field_b.at[0], STEP_TIME / 4.0, 1)
    run(field_b.at[0], field_b.at[1], STEP_TIME / 3.0, 2)
    run(field_b.at[1], field_b.at[0], STEP_TIME / 2.0, 3)
    run(field_b.at[0], out_v, STEP_TIME, 4, True)
    wave_copy = pltpu.make_async_copy(out_v, wave_out, out_sem.at[1])
    wave_copy.start()

    left_behind(send1, 0)
    left_behind(send2, 1)
    left_behind(send3, 2)
    for copy in gathers + margin:
        copy.wait_send()
    pot_copy.wait()
    wave_copy.wait()


def body(wave, offsets, waves, amps, widths, tile, send_list, send_count):
    given = (
        wave,
        offsets.reshape(3, 1, BEAMS),
        waves.reshape(3, 1, BEAMS),
        amps.reshape(2, 1, BEAMS),
        widths.reshape(1, BEAMS),
        tile.reshape(1, BEAMS),
        send_list.reshape(1, BEAMS),
        send_count.reshape(1, G),
    )
    tabs = tuple(jnp.asarray(t) for t in tables())
    row = (G, 1, 128)
    anywhere = pl.BlockSpec(memory_space=pl.ANY)
    dma = pltpu.SemaphoreType.DMA
    scratch = [pltpu.VMEM(shape, kind) for shape, kind in ARG_SHAPES]
    scratch += [pltpu.VMEM(shape, F32) for shape in TAB_SHAPES]
    scratch += [
        pltpu.VMEM((16, BEAMS), F32),
        pltpu.VMEM((128, 128), F32),
        pltpu.VMEM((128, 128), F32),
    ]
    scratch += [pltpu.VMEM(row, F32)] * 6
    scratch += [pltpu.VMEM((16, 256), F32), pltpu.VMEM((M, 16, 256), F32)]
    scratch += [pltpu.VMEM((256, SLOTS * 256), BF16)] * 4
    scratch += [
        pltpu.VMEM((2, 2 * COLS, 128), F32),
        pltpu.VMEM((6, 2, EXT_X, 128), F32),
        pltpu.VMEM((2, EXT_Z, EXT_X, NY), F32),
        pltpu.VMEM((2, 2, EXT_Z, EXT_X, NY), F32),
        pltpu.VMEM((2, PLANES, COLS, NY), F32),
        pltpu.VMEM((2, 16, 128), F32),
    ]
    scratch += [
        dma((N_ARG,)), dma((N_TAB,)), dma((2,)), dma((3,)), dma((3,)),
        dma((M,)), dma((M,)), dma((8,)), dma((8,)),
    ]
    return pl.pallas_call(
        kernel,
        out_shape=(
            jax.ShapeDtypeStruct((2, PLANES, COLS, NY), F32),
            jax.ShapeDtypeStruct((2, 16, 128), F32),
        ),
        in_specs=[anywhere] * (N_ARG + N_TAB),
        out_specs=(anywhere, anywhere),
        scratch_shapes=scratch,
        compiler_params=pltpu.CompilerParams(
            collective_id=0, has_side_effects=True, vmem_limit_bytes=48 * 1024 * 1024
        ),
    )(*given, *tabs)


def solution(mesh):
    line = P("grp", "mem", None)
    stacked = P(None, "grp", "mem", None)
    return jax.shard_map(
        body,
        mesh=mesh,
        in_specs=(stacked, stacked, stacked, stacked, line, line, line, line),
        out_specs=(stacked, line),
        check_vma=False,
    )
```

```python
import functools
import math

import jax
import jax.numpy as jnp
import numpy as np
from jax import lax
from jax.experimental import pallas as pl
from jax.experimental.pallas import tpu as pltpu
from jax.sharding import PartitionSpec as P


F32 = jnp.float32
BF16 = jnp.bfloat16
HIGHEST = lax.Precision.HIGHEST
MESH = pl.DeviceIdType.MESH

GRAV = 0.005
SCREEN = 0.0004
STEP_TIME = 0.2

G = 128
M = 8
SLOTS = 8
PLANES = 4
COLS = 32
NY = 256
BEAMS = 1024
PAD = 8
EXT_Z = PLANES + 8
EXT_X = COLS + 2 * PAD
PLANE_ROWS = ((0, 0, 24), (1, 24, 24), (-1, 48, 24), (2, 72, 24), (-2, 96, 16), (3, 112, 16))


def basis(number):
    half = number // 2
    at = np.arange(number)
    waves = np.concatenate([np.arange(half + 1), np.arange(1, half)])
    angles = 2.0 * np.pi / number * (waves[:, None] * at[None, :] % number)
    vectors = np.where(np.arange(number)[:, None] <= half, np.cos(angles), np.sin(angles))
    return vectors, (vectors**2).sum(1), 2.0 * np.cos(2.0 * np.pi / number * waves) - 2.0


@functools.cache
def tables():
    vec_y, len_y, eig_y = basis(128)
    vec_x, len_x, eig_x = vec_y, len_y, eig_y
    wz = np.arange(128)
    at = np.arange(256)
    ang = 2.0 * np.pi / 256 * (wz[:, None] * at[None, :] % 256)
    second = np.sin(ang)
    second[0] = np.cos(np.pi * at)
    vec_z = np.concatenate([np.cos(ang), second])
    len_z = (vec_z**2).sum(1)
    lam = 2.0 * np.cos(2.0 * np.pi / 256 * wz) - 2.0
    lam_second = lam.copy()
    lam_second[0] = -4.0
    eig_z = np.concatenate([lam, lam_second])

    fwd_y = np.repeat(vec_y, 2, axis=1)
    fwd_z = np.concatenate([vec_z[:, 0::2], vec_z[:, 1::2]], axis=1).T
    fwd_x = vec_x
    inv_x = np.zeros((128, 128))
    shift = np.zeros(128)
    for offset, first, rows in PLANE_ROWS:
        margin = (rows - 16) // 2
        where = (np.arange(rows) - margin) % 128
        inv_x[first : first + rows] = (vec_x / len_x[:, None])[:, where].T
        shift[first : first + rows] = offset
    turn = 2.0 * np.pi / 256 * wz[None, :] * shift[:, None]
    rot_c, rot_s = np.cos(turn), np.sin(turn)
    rot_d = rot_c.copy()
    rot_d[:, 0] = np.cos(np.pi * shift)
    inv_z = (vec_z / len_z[:, None])[:, 0::2].T
    inv_y = (vec_y / len_y[:, None]).copy()
    inv_y = np.concatenate([np.repeat(inv_y, 2, axis=1), inv_y], axis=1)
    lam_xz = eig_x[:, None] + eig_z[None, :] - SCREEN
    lam_y = np.broadcast_to(eig_y[:, None, None], (128, 1, 256))
    many = (fwd_y, fwd_z, fwd_x, inv_x, rot_c, rot_s, rot_d, inv_z, inv_y, lam_xz, lam_y)
    return tuple(np.ascontiguousarray(t, dtype=np.float32) for t in many)


SIN = tuple((-1.0) ** i / math.factorial(2 * i + 1) for i in range(6))
COS = tuple((-1.0) ** i / math.factorial(2 * i) for i in range(7))
TURN_HIGH = 6.28125
TURN_LOW = 2.0 * math.pi - TURN_HIGH


def cos_sin(phase):
    turns = jnp.round(phase * (0.5 / math.pi))
    half = 0.5 * ((phase - turns * TURN_HIGH) - turns * TURN_LOW)
    square = half * half
    sine = SIN[-1]
    for c in SIN[-2::-1]:
        sine = sine * square + c
    sine = sine * half
    cosine = COS[-1]
    for c in COS[-2::-1]:
        cosine = cosine * square + c
    return 1.0 - 2.0 * (sine * sine), 2.0 * (sine * cosine)


def parts(value):
    high = value.astype(BF16)
    return high, (value - high.astype(F32)).astype(BF16)


def dot(a, b):
    return jnp.dot(a, b, precision=HIGHEST, preferred_element_type=F32)


def dot_t(a, b, precision=HIGHEST):
    dims = (((1,), (1,)), ((), ()))
    return lax.dot_general(a, b, dims, precision=precision, preferred_element_type=F32)


def iota(shape, dim):
    return lax.broadcasted_iota(jnp.int32, shape, dim)


N_TAB = 11
TAB_SHAPES = (
    (128, 256), (256, 256), (128, 128), (128, 128), (128, 128), (128, 128), (128, 128),
    (128, 256), (128, 384), (128, 256), (1, 256),
)
ARG_SHAPES = (
    ((2, PLANES, COLS, NY), F32), ((3, 1, BEAMS), F32), ((3, 1, BEAMS), F32), ((2, 1, BEAMS), F32),
    ((1, BEAMS), F32), ((1, BEAMS), jnp.int32), ((1, BEAMS), jnp.int32), ((1, G), jnp.int32),
)
N_ARG = len(ARG_SHAPES)


def kernel(*refs):
    args_hbm, refs = refs[:N_ARG], refs[N_ARG:]
    tabs_hbm, refs = refs[:N_TAB], refs[N_TAB:]
    wave_out, pot_out = refs[:2]
    refs = refs[2:]
    args_v, refs = refs[:N_ARG], refs[N_ARG:]
    tabs_v, refs = refs[:N_TAB], refs[N_TAB:]
    (
        rows_v, one_v, two_v, send1, recv1, send2, recv2, send3, recv3, own_x, all_x,
        left_h, left_l, right_h, right_l, dens_v, pot_v, field_a, field_b, out_v, pot_c,
        arg_sem, tab_sem, out_sem, s_sem, r_sem, xs_sem, xr_sem, hs_sem, hr_sem,
    ) = refs
    wave_v, off_v, wav_v, amp_v, wid_v, til_v, sl_v, cnt_v = args_v
    (fwd_y, fwd_z, fwd_x, inv_x, rot_c, rot_s, rot_d, inv_z, inv_y, lam_xz, lam_y) = tabs_v

    g = lax.axis_index("grp")
    m = lax.axis_index("mem")
    barrier = pltpu.get_barrier_semaphore()

    def greet(j, carry):
        pl.semaphore_signal(
            barrier, inc=1, device_id=(lax.rem(g + j, G), m), device_id_type=MESH
        )
        return carry

    lax.fori_loop(1, G, greet, 0)
    for j in range(1, M):
        pl.semaphore_signal(
            barrier, inc=1, device_id=(g, lax.rem(m + j, M)), device_id_type=MESH
        )
    up, down = lax.rem(g + 1, G), lax.rem(g + G - 1, G)
    right, left = lax.rem(m + 1, M), lax.rem(m + M - 1, M)
    for corner in ((up, right), (up, left), (down, right), (down, left)):
        pl.semaphore_signal(barrier, inc=1, device_id=corner, device_id_type=MESH)

    arg_copies = [
        pltpu.make_async_copy(args_hbm[i], args_v[i], arg_sem.at[i]) for i in range(N_ARG)
    ]
    for i in (6, 5, 1, 2, 3, 4, 7, 0):
        arg_copies[i].start()
    tab_copies = []
    for i in range(N_TAB):
        source = tabs_hbm[i].at[g] if i == N_TAB - 1 else tabs_hbm[i]
        tab_copies.append(pltpu.make_async_copy(source, tabs_v[i], tab_sem.at[i]))
        tab_copies[i].start()

    arg_copies[6].wait()
    listed = jnp.broadcast_to(sl_v[...], (SLOTS, BEAMS))
    mine = (iota((SLOTS, BEAMS), 1) & (SLOTS - 1)) == iota((SLOTS, BEAMS), 0)
    listed = jnp.concatenate(
        [jnp.where(mine, listed >> 5, 0), jnp.where(mine, listed & 31, 0)], axis=0
    )
    spread = (iota((BEAMS, G), 0) >> 3) == iota((BEAMS, G), 1)
    found = jnp.dot(
        listed.astype(F32).astype(BF16),
        jnp.where(spread, 1.0, 0.0).astype(BF16),
        preferred_element_type=F32,
    )
    by_slot = (found[:SLOTS] * 32.0 + found[SLOTS:]).astype(jnp.int32)

    for i in (1, 2, 3, 4, 5, 7):
        arg_copies[i].wait()
    tile = til_v[...]
    rows_v[...] = jnp.zeros_like(rows_v)
    rows_v[0:1, :] = off_v[0] * float(PLANES)
    rows_v[1:2, :] = 16.0 * (tile >> 4).astype(F32) + 16.0 * off_v[1]
    rows_v[2:3, :] = 16.0 * (tile & 15).astype(F32) + 16.0 * off_v[2]
    for d in range(3):
        rows_v[3 + d : 4 + d, :] = wav_v[d]
    rows_v[6:7, :] = amp_v[0]
    rows_v[7:8, :] = amp_v[1]
    rows_v[8:9, :] = wid_v[...]
    exact = rows_v[...]
    first, rest = parts(exact)
    second = rest
    third = ((exact - first.astype(F32)) - second.astype(F32)).astype(BF16)
    three = jnp.concatenate([first, second, third], axis=0)
    for c in range(SLOTS):
        chosen = iota((BEAMS, G), 0) == by_slot[c : c + 1, :]
        picked = jnp.dot(
            three, jnp.where(chosen, 1.0, 0.0).astype(BF16), preferred_element_type=F32
        )
        one_v[pl.ds(c, 16, stride=SLOTS), :] = picked[0:16] + picked[16:32] + picked[32:48]
    filled = iota((SLOTS, G), 0) < cnt_v[...]
    for p in (6, 7):
        rows = slice(p * SLOTS, (p + 1) * SLOTS)
        one_v[rows, :] = jnp.where(filled, one_v[rows, :], 0.0)
    send1[:, 0, :] = one_v[...].T

    pl.semaphore_wait(barrier, (G - 1) + (M - 1) + 4)

    def scatter(source, target, number):
        def one(j, carry):
            h = lax.rem(g + j, G)
            pltpu.make_async_remote_copy(
                src_ref=source.at[h],
                dst_ref=target.at[g],
                send_sem=s_sem.at[number],
                recv_sem=r_sem.at[number],
                device_id=(h, m),
                device_id_type=MESH,
            ).start()
            return carry

        lax.fori_loop(1, G, one, 0)
        target[g] = source[g]

    def others(ref):
        return ref.at[pl.ds(0, G - 1)]

    def arrived(target, number):
        pltpu.make_async_copy(others(target), others(target), r_sem.at[number]).wait()

    def left_behind(source, number):
        pltpu.make_async_copy(others(source), others(source), s_sem.at[number]).wait()

    scatter(send1, recv1, 0)
    arrived(recv1, 0)

    two_v[...] = recv1[:, 0, :].T

    def profiles(c, carry):
        def row(p):
            return two_v[pl.ds(p * SLOTS + c, 1), :]

        width = row(8)
        scale = -0.5 / (width * width)
        at = pl.multiple_of(c * 256, 256)
        low, high = pl.ds(at, 128), pl.ds(at + 128, 128)

        away = iota((8, G), 0).astype(F32) - row(0)
        bell = jnp.exp(away * away * scale)
        cosine, sine = cos_sin(row(3) * away)
        z_r, z_i = bell * cosine, bell * sine
        a_r, a_i = row(6), row(7)
        az_r, az_i = a_r * z_r - a_i * z_i, a_r * z_i + a_i * z_r

        away = iota((COLS, G), 0).astype(F32) - row(1)
        bell = jnp.exp(away * away * scale)
        cosine, sine = cos_sin(row(4) * away)
        x_r, x_i = bell * cosine, bell * sine
        for z in range(PLANES):
            p_r, p_i = az_r[z : z + 1], az_i[z : z + 1]
            real, imag = p_r * x_r - p_i * x_i, p_r * x_i + p_i * x_r
            real_h, real_l = parts(real)
            imag_h, imag_l = parts(imag)
            top = slice(z * COLS, (z + 1) * COLS)
            bottom = slice(128 + z * COLS, 128 + (z + 1) * COLS)
            left_h[top, low] = real_h
            left_l[top, low] = real_l
            left_h[top, high] = -imag_h
            left_l[top, high] = -imag_l
            left_h[bottom, low] = imag_h
            left_l[bottom, low] = imag_l
            left_h[bottom, high] = real_h
            left_l[bottom, high] = real_l

        c_y, k_y = row(2), row(5)
        step = iota((16, G), 0).astype(F32)
        coarse_c, coarse_s = cos_sin(k_y * (16.0 * step - c_y))
        fine_c, fine_s = cos_sin(k_y * step)
        for a in range(16):
            away = (step + 16.0 * a) - c_y
            bell = jnp.exp(away * away * scale)
            b_c, b_s = coarse_c[a : a + 1], coarse_s[a : a + 1]
            real_h, real_l = parts(bell * (b_c * fine_c - b_s * fine_s))
            imag_h, imag_l = parts(bell * (b_s * fine_c + b_c * fine_s))
            rows = slice(16 * a, 16 * a + 16)
            right_h[rows, low] = real_h
            right_l[rows, low] = real_l
            right_h[rows, high] = imag_h
            right_l[rows, high] = imag_l
        return carry

    lax.fori_loop(0, SLOTS, profiles, 0)
    deposited = (
        dot_t(left_h[...], right_h[...], None)
        + dot_t(left_l[...], right_h[...], None)
        + dot_t(left_h[...], right_l[...], None)
    )
    arg_copies[0].wait()
    own_z, own_cols = pl.ds(4, PLANES), pl.ds(PAD, COLS)
    for z in range(PLANES):
        for part in range(2):
            rows = slice(part * 128 + z * COLS, part * 128 + (z + 1) * COLS)
            field_a[part, 4 + z, own_cols, :] = wave_v[part, z] + deposited[rows]
    for z in range(2):
        total = None
        for plane in (4 + 2 * z, 5 + 2 * z):
            for part in range(2):
                value = field_a[part, plane, own_cols, :]
                total = value * value if total is None else total + value * value
        for side in range(2):
            dens_v[side, z * COLS : (z + 1) * COLS, :] = total[:, side * 128 : (side + 1) * 128]
    pooled = [
        dens_v[side, pl.ds(0, COLS, stride=2), :] + dens_v[side, pl.ds(1, COLS, stride=2), :]
        for side in range(2)
    ]
    pooled = jnp.concatenate(pooled, axis=1)

    for copy in tab_copies:
        copy.wait()
    pooled = jnp.concatenate([pooled, jnp.zeros((96, NY), F32)], axis=0)
    send2[:, 0, :] = dot_t(fwd_y[...], pooled)
    scatter(send2, recv2, 1)

    first_cols, last_cols = pl.ds(PAD, 8), pl.ds(PAD + COLS - 8, 8)
    low_cols, high_cols = pl.ds(0, 8), pl.ds(PAD + COLS, 8)
    low_z, high_z = pl.ds(0, 4), pl.ds(8, 4)
    margin = []
    for i, (who, there_z, here_x, there_x) in enumerate(
        (
            ((up, m), low_z, own_cols, own_cols),
            ((down, m), high_z, own_cols, own_cols),
            ((g, right), own_z, last_cols, low_cols),
            ((g, left), own_z, first_cols, high_cols),
            ((up, right), low_z, last_cols, low_cols),
            ((up, left), low_z, first_cols, high_cols),
            ((down, right), high_z, last_cols, low_cols),
            ((down, left), high_z, first_cols, high_cols),
        )
    ):
        copy = pltpu.make_async_remote_copy(
            src_ref=field_a.at[:, own_z, here_x, :],
            dst_ref=field_a.at[:, there_z, there_x, :],
            send_sem=hs_sem.at[i],
            recv_sem=hr_sem.at[i],
            device_id=who,
            device_id_type=MESH,
        )
        copy.start()
        margin.append(copy)

    arrived(recv2, 1)
    turned = recv2[:, 0, :].T
    columns = jnp.concatenate([turned[0:16], turned[16:32]], axis=1)
    spectrum = dot(columns, fwd_z[...])
    own_x[...] = spectrum
    gathers = []
    for j in range(1, M):
        copy = pltpu.make_async_remote_copy(
            src_ref=own_x,
            dst_ref=all_x.at[j],
            send_sem=xs_sem.at[j],
            recv_sem=xr_sem.at[j],
            device_id=(g, lax.rem(m + M - j, M)),
            device_id_type=MESH,
        )
        copy.start()
        gathers.append(copy)
    all_x[0] = spectrum
    zero_mode = (iota((128, 256), 0) == 0) & (iota((128, 256), 1) == 0) & (g == 0)
    factor = jnp.where(zero_mode, 0.0, (GRAV / 8.0) / (lam_xz[...] + lam_y[...]))
    for copy in gathers:
        copy.wait_recv()
    filtered = dot(fwd_x[...], all_x[...].reshape(128, 256)) * factor
    wanted = dot(inv_x[...], filtered)
    even, odd = wanted[:, :128], wanted[:, 128:]
    moved = jnp.concatenate(
        [rot_c[...] * even + rot_s[...] * odd, rot_d[...] * odd - rot_s[...] * even], axis=1
    )
    send3[:, 0, :] = dot_t(inv_z[...], moved)
    scatter(send3, recv3, 2)
    arrived(recv3, 2)

    pot_wide = dot(recv3[:, 0, :].T, inv_y[...])
    pot_c[0] = pot_wide[4:20, NY:]
    pot_c[1] = pot_wide[28:44, NY:]
    pot_copy = pltpu.make_async_copy(pot_c, pot_out, out_sem.at[0])
    pot_copy.start()
    for edge in (0, 5):
        pot_v[edge] = jnp.full((2, EXT_X, 128), 3.0, F32)
    for offset, start, rows in PLANE_ROWS:
        block = pot_wide[start : start + rows, :NY] + 3.0
        skip = (24 - rows) // 2 * 2
        for odd_row in range(2):
            for side in range(2):
                half = block[:, side * 128 : (side + 1) * 128]
                pot_v[offset + 2, side, pl.ds(skip + odd_row, rows, stride=2), :] = half

    for copy in margin:
        copy.wait_recv()

    def stage(source, target, length, z, rows):
        top = 0 if rows is None else PAD
        count = EXT_X if rows is None else COLS
        keep = pl.ds(top, count)
        three_plus = jnp.concatenate(
            [pot_v[z // 2, 0, keep, :], pot_v[z // 2, 1, keep, :]], axis=1
        )
        sums, centres = [], []
        for part in range(2):
            whole = source[part, z]
            beside = pltpu.roll(whole, 1, 0) + pltpu.roll(whole, EXT_X - 1, 0)
            centre = source[part, z, keep, :]
            total = (
                (source[part, z - 1, keep, :] + source[part, z + 1, keep, :])
                + beside[top : top + count]
                + (pltpu.roll(centre, 1, 1) + pltpu.roll(centre, NY - 1, 1))
            )
            sums.append(0.5 * total)
            centres.append(centre)
        real = three_plus * centres[1] - sums[1]
        imag = sums[0] - three_plus * centres[0]
        new_real = field_a[0, z, keep, :] + length * real
        new_imag = field_a[1, z, keep, :] + length * imag
        if rows is None:
            target[0, z] = new_real
            target[1, z] = new_imag
        else:
            target[0, z - 4] = new_real
            target[1, z - 4] = new_imag


    def run(source, target, length, margin_z, rows=None):
        def one(z, carry):
            stage(source, target, length, z, rows)
            return carry

        lax.fori_loop(margin_z, EXT_Z - margin_z, one, 0)

    run(field_a, field_b.at[0], STEP_TIME / 4.0, 1)
    run(field_b.at[0], field_b.at[1], STEP_TIME / 3.0, 2)
    run(field_b.at[1], field_b.at[0], STEP_TIME / 2.0, 3)
    run(field_b.at[0], out_v, STEP_TIME, 4, True)
    wave_copy = pltpu.make_async_copy(out_v, wave_out, out_sem.at[1])
    wave_copy.start()

    left_behind(send1, 0)
    left_behind(send2, 1)
    left_behind(send3, 2)
    for copy in gathers + margin:
        copy.wait_send()
    pot_copy.wait()
    wave_copy.wait()


def body(wave, offsets, waves, amps, widths, tile, send_list, send_count):
    given = (
        wave,
        offsets.reshape(3, 1, BEAMS),
        waves.reshape(3, 1, BEAMS),
        amps.reshape(2, 1, BEAMS),
        widths.reshape(1, BEAMS),
        tile.reshape(1, BEAMS),
        send_list.reshape(1, BEAMS),
        send_count.reshape(1, G),
    )
    tabs = tuple(jnp.asarray(t) for t in tables())
    row = (G, 1, 128)
    anywhere = pl.BlockSpec(memory_space=pltpu.HBM)
    dma = pltpu.SemaphoreType.DMA
    scratch = [pltpu.VMEM(shape, kind) for shape, kind in ARG_SHAPES]
    scratch += [pltpu.VMEM(shape, F32) for shape in TAB_SHAPES]
    scratch += [
        pltpu.VMEM((16, BEAMS), F32),
        pltpu.VMEM((128, 128), F32),
        pltpu.VMEM((128, 128), F32),
    ]
    scratch += [pltpu.VMEM(row, F32)] * 6
    scratch += [pltpu.VMEM((16, 256), F32), pltpu.VMEM((M, 16, 256), F32)]
    scratch += [pltpu.VMEM((256, SLOTS * 256), BF16)] * 4
    scratch += [
        pltpu.VMEM((2, 2 * COLS, 128), F32),
        pltpu.VMEM((6, 2, EXT_X, 128), F32),
        pltpu.VMEM((2, EXT_Z, EXT_X, NY), F32),
        pltpu.VMEM((2, 2, EXT_Z, EXT_X, NY), F32),
        pltpu.VMEM((2, PLANES, COLS, NY), F32),
        pltpu.VMEM((2, 16, 128), F32),
    ]
    scratch += [
        dma((N_ARG,)), dma((N_TAB,)), dma((2,)), dma((3,)), dma((3,)),
        dma((M,)), dma((M,)), dma((8,)), dma((8,)),
    ]
    return pl.pallas_call(
        kernel,
        out_shape=(
            jax.ShapeDtypeStruct((2, PLANES, COLS, NY), F32),
            jax.ShapeDtypeStruct((2, 16, 128), F32),
        ),
        in_specs=[anywhere] * (N_ARG + N_TAB),
        out_specs=(anywhere, anywhere),
        scratch_shapes=scratch,
        compiler_params=pltpu.CompilerParams(
            collective_id=0, has_side_effects=True, vmem_limit_bytes=67043328
        ),
    )(*given, *tabs)


def solution(mesh):
    line = P("grp", "mem", None)
    stacked = P(None, "grp", "mem", None)
    return jax.shard_map(
        body,
        mesh=mesh,
        in_specs=(stacked, stacked, stacked, stacked, line, line, line, line),
        out_specs=(stacked, line),
        check_vma=False,
    )
```
